256 devices in a mesh: occ: 16 (over z_lo, y), aux: 16 (over z_hi, x, core).
Axes of the slice: x: 4, y: 4, z: 8 (z_hi: 2, z_lo: 4; z = z_hi * 4 + z_lo), core: 2. Of those that a mesh axis runs over, the one named last changes fastest.
Arguments:
- factors: bfloat16 [8192, 32, 1024], P('aux', 'occ'), may hold values from -16 to 16
- partner: bfloat16 [8192, 1024], P('aux', 'occ'), may hold values from -0.09375 to 0.09375
- occupied_energy: float32 [32], P('occ'), may hold values from -2 to -0.5
- partner_energy: float32 [1], replicated, may hold values from -3 to -0.3
- virtual_energy: float32 [1024], replicated, may hold values from 0.2 to 3
Outputs:
- amplitudes: bfloat16 [32768, 1024], P(('occ', 'aux'))
- density_factors: bfloat16 [8192, 32, 1024], P('aux', 'occ')
The draws below stay inside these ranges and needn't reach their ends.
All inputs are finite; a program needn't handle non-finite values.
Results may differ from the reference program's by a relative error of at most 0.015.
Values may be sent and summed in bfloat16 or wider, within the bound.
A program may use at most 64 MiB of HBM per device.

```python
import jax
import jax.numpy as jnp
from jax import lax

V = 1024
Q_DEV = 512
OCC = 32
Q = 8192
N_AUX = 16


def levels(key, shape, shards, low, high):
    def one(position, shards_of):
        draws = jax.random.uniform(jax.random.fold_in(jax.random.fold_in(key, 6), position), (shards_of,), jnp.float32, low / len(shards), high / len(shards))
        return jnp.repeat(jnp.exp(draws), shape[position] // shards_of).reshape((-1,) + (1,) * (len(shape) - position - 1))

    loudness = one(*shards[0])
    for cut in shards[1:]:
        loudness = loudness * one(*cut)
    return loudness


def bell_draw(rng, dims, spread, reach, cuts=(), held_as=jnp.bfloat16):
    gain = levels(rng, dims, cuts, -0.22, 0.18) if cuts else 1.0
    entries = jax.random.normal(rng, dims, jnp.float32) * spread * gain
    return jnp.minimum(jnp.maximum(entries, -reach), reach).astype(held_as)


def setup_inputs(seed: int = 0) -> dict:
    key_of = jax.random.split(jax.random.key(seed), 6)
    return {
        "factors": bell_draw(key_of[0], (Q, OCC, V), (8 * (V / Q) ** 0.5), 16.0, ((0, 16), (1, 16))),
        "partner": bell_draw(key_of[1], (Q, V), (0.5 / V ** 0.5), 0.09375, ((0, 16), (1, 16))),
        "occupied_energy": jnp.clip(-2.0 + 1.5 * jax.random.uniform(key_of[2], (OCC,), jnp.float32) ** levels(key_of[2], (OCC,), ((0, 16),), -0.2, 0.2), -2.0, -0.5),
        "partner_energy": jnp.clip(jax.random.uniform(key_of[3], (1,), jnp.float32, -3.0, -0.3), -3.0, -0.3),
        "virtual_energy": jnp.clip(jax.random.uniform(key_of[4], (V,), jnp.float32, 0.2, 3.0), 0.2, 3.0),
    }


def reference(factors, partner, occupied_energy, partner_energy, virtual_energy):
    occ_total = factors.shape[1]
    virt_count = factors.shape[2]
    factor_blocks = factors.reshape(N_AUX, Q_DEV, occ_total * virt_count)
    partner_blocks = partner.reshape(N_AUX, Q_DEV, virt_count)

    def add_block(carry, pieces):
        block_rows, block_cols = pieces
        partial_sum = lax.dot_general(block_rows.astype(jnp.float32), block_cols.astype(jnp.float32), (((0,), (0,)), ((), ())), precision=lax.Precision.HIGHEST)
        rounded = lax.optimization_barrier(partial_sum.astype(jnp.bfloat16))
        return carry + rounded.astype(jnp.float32), None

    start_sum = jnp.zeros((occ_total * virt_count, virt_count), jnp.float32)
    integrals, _ = lax.scan(add_block, start_sum, (factor_blocks, partner_blocks))
    occ_rows = jnp.repeat(occupied_energy, virt_count)
    virt_rows = jnp.tile(virtual_energy, occ_total)
    divisor = virt_rows[:, None] + virtual_energy[None, :] - occ_rows[:, None] - partner_energy[0]
    amplitudes = (-integrals / divisor).astype(jnp.bfloat16)
    amp_cube = amplitudes.reshape(occ_total, virt_count, virt_count)
    partner_wide = partner.astype(jnp.float32)

    def one_orbital(amp_block):
        block_wide = amp_block.astype(jnp.float32)
        direct = jnp.dot(partner_wide, block_wide.T, precision=lax.Precision.HIGHEST)
        swapped = jnp.dot(partner_wide, block_wide, precision=lax.Precision.HIGHEST)
        return (2.0 * direct - swapped).astype(jnp.bfloat16)

    density = lax.map(one_orbital, amp_cube)
    return amplitudes, jnp.transpose(density, (1, 0, 2))
```

```python
import jax
import jax.numpy as jnp
from jax import lax
from jax.experimental import pallas as pl
from jax.experimental.pallas import tpu as pltpu
from jax.sharding import PartitionSpec as P

MESH = pl.DeviceIdType.MESH
NX, NY, NZ = 4, 4, 4
BLK = 128

PZ = 0
PYP = 4
PYM = 8
PYF = 12
PS = 16
FS = 20
R1 = 24
R2 = 32
RZ = 48
GZ = 52
GX = 56
GF = 72
GS = 80
NSEM = 84


def kernel(
    f_ref, pt_ref, occ_ref, pe_ref, ve_ref,
    amp_ref, den_ref,
    ptb, fr, part, rx1, rx2, keep, zr, at, vcol, ptrue, ss, rs,
):
    o, u = lax.axis_index("occ"), lax.axis_index("aux")
    zl, y = o // NY, o % NY
    zh, x, c = u // (2 * NX), (u // 2) % NX, u % 2

    def up(k):
        return (y + k) % NY

    def dev(dzh=0, dzl=0, dy=0, dx=0, dc=0):
        return (
            ((zl + dzl) % NZ) * NY + (y + dy) % NY,
            (((zh + dzh) % 2) * NX + (x + dx) % NX) * 2 + (c + dc) % 2,
        )

    sib, zpart = dev(dc=1), dev(dzh=1)
    xp, xm = dev(dx=1), dev(dx=NX - 1)
    yp, ym = dev(dy=1), dev(dy=NY - 1)
    sent = []

    def copy(src, dst, sem, to):
        return pltpu.make_async_remote_copy(
            src_ref=src, dst_ref=dst, send_sem=ss.at[sem], recv_sem=rs.at[sem],
            device_id=to, device_id_type=MESH,
        )

    def send(src, dst, sem, to):
        cp = copy(src, dst, sem, to)
        cp.start()
        sent.append(cp)

    def arrive(dst, sem, frm):
        copy(dst, dst, sem, frm).wait_recv()

    barrier = pltpu.get_barrier_semaphore()
    greet = [sib, zpart, xp, xm, yp, ym] + [dev(dzl=k) for k in range(1, NZ)]
    for to in greet:
        pl.semaphore_signal(barrier, inc=1, device_id=to, device_id_type=MESH)
    pl.semaphore_wait(barrier, len(greet))

    def pblock(k, row):
        return ptb.at[c, (zl + NZ - k) % NZ, row]

    for k in range(1, NZ):
        send(pt_ref, pblock(0, y), PZ + k, dev(dzl=k))
    send(pt_ref, pblock(0, y), PYP, yp)
    send(pt_ref, pblock(0, y), PYM, ym)
    send(f_ref.at[1 - c], fr, FS, sib)
    ptb[c, zl, y] = pt_ref[...]

    for z in range(NZ):
        row = jnp.broadcast_to(ve_ref[:, z * 256:(z + 1) * 256], (BLK, 256))
        col = row.T
        for j in range(NY):
            vcol[j, z * 64:(z + 1) * 64, :] = col[j * 64:(j + 1) * 64]
    vrow = ve_ref[:, pl.ds(pl.multiple_of((x * 2 + c) * BLK, BLK), BLK)]
    shift = occ_ref[zh] + pe_ref[0]

    for k in range(1, NZ):
        arrive(pblock(k, y), PZ + k, dev(dzl=NZ - k))
        send(pblock(k, y), pblock(k, y), PYP + k, yp)
        send(pblock(k, y), pblock(k, y), PYM + k, ym)

    order = [0, 1, NY - 1, 2]
    chunk_of = [up(k) for k in order]

    def to_sibling(t):
        row = chunk_of[t]
        send(ptb.at[c, :, row], ptb.at[c, :, row], PS + t, sib)

    def partner_sides():
        for k in range(NZ):
            arrive(pblock(k, up(NY - 1)), PYP + k, ym)
            arrive(pblock(k, up(1)), PYM + k, yp)
            if k < NZ // 2:
                b = pblock(k, up(NY - 1))
                send(b, b, PYF + k, yp)
            else:
                b = pblock(k, up(1))
                send(b, b, PYF + k, ym)

    def partner_far():
        for k in range(NZ):
            arrive(pblock(k, up(2)), PYF + k, ym if k < NZ // 2 else yp)

    def spot(h, dx):
        return h * NX + (x + dx) % NX

    def partial(t):
        row = chunk_of[t]
        arrive(ptb.at[1 - c, :, row], PS + t, sib)

        @pl.loop(0, 4)
        def _(pair):
            mine = ptb[c, :, row].reshape(256, 512)
            other = ptb[1 - c, :, row].reshape(256, 512)
            f_mine = jnp.concatenate([f_ref[c, 2 * pair], f_ref[c, 2 * pair + 1]], axis=1)
            f_other = jnp.concatenate([fr[2 * pair], fr[2 * pair + 1]], axis=1)
            total = jnp.dot(mine, f_mine, preferred_element_type=jnp.float32)
            total += jnp.dot(other, f_other, preferred_element_type=jnp.float32)
            total = total.astype(jnp.bfloat16)
            part[t, 2 * pair] = total[:, :BLK]
            part[t, 2 * pair + 1] = total[:, BLK:]

        send(part.at[t, spot(0, 2)], rx1.at[t, 0], R1 + 2 * t, xp)
        send(part.at[t, spot(1, 2)], rx1.at[t, 1], R1 + 2 * t + 1, xm)
        send(part.at[t, spot(1, 1)], rx2.at[t, 1], R2 + 4 * t + 1, xp)
        send(part.at[t, spot(0, NX - 1)], rx2.at[t, 2], R2 + 4 * t + 2, xm)

    def combine(t):
        for h, dx, to, frm, slot in ((0, 1, xp, xm, 0), (1, NX - 1, xm, xp, 3)):
            arrive(rx1.at[t, h], R1 + 2 * t + h, frm)
            m = spot(h, dx)
            both = part[t, m].astype(jnp.float32) + rx1[t, h].astype(jnp.float32)
            part[t, m] = both.astype(jnp.bfloat16)
            send(part.at[t, m], rx2.at[t, slot], R2 + 4 * t + slot, to)

    def over_x(t):
        for slot in range(4):
            arrive(rx2.at[t, slot], R2 + 4 * t + slot, xm if slot < 2 else xp)

        def total(h):
            return (
                part[t, spot(h, 0)].astype(jnp.float32)
                + rx2[t, h].astype(jnp.float32)
                + rx2[t, 2 + h].astype(jnp.float32)
            )

        part[t, spot(1 - zh, 0)] = total(1 - zh).astype(jnp.bfloat16)
        send(part.at[t, spot(1 - zh, 0)], zr.at[t], RZ + t, zpart)
        keep[t] = total(zh)

    step = 1 - 2 * zh

    def ablock(h, dx, row):
        return at.at[c, spot(h, dx), :, row]

    def amplitude(t):
        row = chunk_of[t]
        arrive(zr.at[t], RZ + t, zpart)
        total = keep[t] + zr[t].astype(jnp.float32)
        divisor = vrow + vcol[row] - shift
        amp = (-total / divisor).astype(jnp.bfloat16)
        at[c, spot(zh, 0), :, row] = amp.reshape(NZ, 64, BLK)
        b = ablock(zh, 0, row)
        send(b, b, GX + 4 * t, xp)
        send(b, b, GX + 4 * t + 1, xm)
        send(b, b, GZ + t, zpart)

    def gather_z(t):
        b = ablock(1 - zh, 0, chunk_of[t])
        arrive(b, GZ + t, zpart)
        send(b, b, GX + 4 * t + 2, xp)
        send(b, b, GX + 4 * t + 3, xm)

    def gather_own(t):
        row = chunk_of[t]
        arrive(ablock(zh, NX - 1, row), GX + 4 * t, xm)
        arrive(ablock(zh, 1, row), GX + 4 * t + 1, xp)
        b = ablock(zh, NX - step, row)
        send(b, b, GF + 2 * t, dev(dx=NX + step))

    def gather_other(t):
        row = chunk_of[t]
        arrive(ablock(1 - zh, NX - 1, row), GX + 4 * t + 2, xm)
        arrive(ablock(1 - zh, 1, row), GX + 4 * t + 3, xp)
        b = ablock(1 - zh, NX + step, row)
        send(b, b, GF + 2 * t + 1, dev(dx=NX - step))

    def gather_end(t):
        row = chunk_of[t]
        arrive(ablock(zh, 2, row), GF + 2 * t, dev(dx=NX - step))
        arrive(ablock(1 - zh, 2, row), GF + 2 * t + 1, dev(dx=NX + step))
        send(at.at[c, :, :, row], at.at[c, :, :, row], GS + t, sib)

    to_sibling(0)
    arrive(fr, FS, sib)
    partial(0)
    partner_sides()
    to_sibling(1)
    to_sibling(2)
    partial(1)
    combine(0)
    partial(2)
    partner_far()
    to_sibling(3)
    combine(1)
    over_x(0)
    partial(3)
    combine(2)
    over_x(1)
    combine(3)

    for z in range(NZ):
        ptrue[:, z * 256:(z + 1) * 256] = ptb[c, z].reshape(256, 512).T

    over_x(2)
    amplitude(0)
    over_x(3)
    amplitude(1)
    gather_z(0)
    gather_own(0)
    amplitude(2)
    gather_z(1)
    gather_own(1)
    amplitude(3)
    gather_other(0)
    gather_z(2)
    gather_own(2)
    gather_other(1)
    gather_end(0)
    gather_z(3)
    gather_own(3)
    gather_other(2)
    gather_end(1)
    for z in range(NZ):
        own = at[c, spot(zh, 0), z].reshape(256, BLK)
        amp_ref[:, z * 256:(z + 1) * 256] = own.T
    gather_other(3)
    gather_end(2)
    gather_end(3)
    for t in range(4):
        row = chunk_of[t]
        arrive(at.at[1 - c, :, :, row], GS + t, sib)

    @pl.loop(0, 2)
    def _(i):
        for z in range(NX):
            wide = jnp.concatenate(
                [at[0, i * NX + z].reshape(1024, BLK), at[1, i * NX + z].reshape(1024, BLK)], axis=1
            )
            direct = jnp.dot(ptrue[...], wide, preferred_element_type=jnp.float32)
            tall = jnp.concatenate(
                [at[j % 2, i * NX + j // 2, z].reshape(256, BLK) for j in range(2 * NX)], axis=1
            )
            swapped = lax.dot_general(
                ptrue[...], tall, (((1,), (1,)), ((), ())), preferred_element_type=jnp.float32
            )
            den_ref[i, :, z * 256:(z + 1) * 256] = (2.0 * direct - swapped).astype(jnp.bfloat16)

    for cp in sent:
        cp.wait_send()


def shards(factors, partner, occupied_energy, partner_energy, virtual_energy):
    split = factors.reshape(512, 8, 2, BLK).transpose(2, 1, 0, 3)
    bf = jnp.bfloat16
    vmem = pl.BlockSpec(memory_space=pltpu.VMEM)
    smem = pl.BlockSpec(memory_space=pltpu.SMEM)
    amp, den = pl.pallas_call(
        kernel,
        out_shape=(jax.ShapeDtypeStruct((BLK, 1024), bf), jax.ShapeDtypeStruct((2, 512, 1024), bf)),
        in_specs=[vmem, vmem, smem, smem, vmem],
        out_specs=(vmem, vmem),
        scratch_shapes=[
            pltpu.VMEM((2, NZ, NY, 64, 512), bf),
            pltpu.VMEM((8, 512, BLK), bf),
            pltpu.VMEM((4, 8, 256, BLK), bf),
            pltpu.VMEM((4, 2, 256, BLK), bf),
            pltpu.VMEM((4, 4, 256, BLK), bf),
            pltpu.VMEM((4, 256, BLK), jnp.float32),
            pltpu.VMEM((4, 256, BLK), bf),
            pltpu.VMEM((2, 8, NZ, NY, 64, BLK), bf),
            pltpu.VMEM((4, 256, BLK), jnp.float32),
            pltpu.VMEM((512, 1024), bf),
            pltpu.SemaphoreType.DMA((NSEM,)),
            pltpu.SemaphoreType.DMA((NSEM,)),
        ],
        compiler_params=pltpu.CompilerParams(
            collective_id=0, has_side_effects=True, vmem_limit_bytes=48 << 20
        ),
    )(split, partner.T, occupied_energy, partner_energy, virtual_energy.reshape(1, 1024))
    return amp, den.transpose(1, 0, 2)


def solution(mesh):
    return jax.shard_map(
        shards,
        mesh=mesh,
        in_specs=(P("aux", "occ", None), P("aux", "occ"), P("occ"), P(), P()),
        out_specs=(P(("occ", "aux"), None), P("aux", "occ", None)),
        check_vma=False,
    )
```

```python
import jax
import jax.numpy as jnp
from jax import lax
from jax.experimental import pallas as pl
from jax.experimental.pallas import tpu as pltpu
from jax.sharding import PartitionSpec as P

MESH = pl.DeviceIdType.MESH
NX, NY, NZ = 4, 4, 4
BLK = 128

PZ = 0
PYP = 4
PYM = 8
PFP = 12
PFM = 16
PS = 20
FS = 24
R1 = 32
R2 = 40
RZ = 56
GZ = 60
GX = 64
GF = 80
GS = 88
NSEM = 92


def kernel(
    f_ref, pt_ref, occ_ref, pe_ref, ve_ref,
    amp_ref, den_ref,
    ptb, fr, part, rx1, rx2, keep, zr, at, vcol, ptrue, ss, rs, near,
):
    o, u = lax.axis_index("occ"), lax.axis_index("aux")
    zl, y = o // NY, o % NY
    zh, x, c = u // (2 * NX), (u // 2) % NX, u % 2

    def up(k):
        return (y + k) % NY

    def dev(dzh=0, dzl=0, dy=0, dx=0, dc=0):
        return (
            ((zl + dzl) % NZ) * NY + (y + dy) % NY,
            (((zh + dzh) % 2) * NX + (x + dx) % NX) * 2 + (c + dc) % 2,
        )

    sib, zpart = dev(dc=1), dev(dzh=1)
    xp, xm = dev(dx=1), dev(dx=NX - 1)
    yp, ym = dev(dy=1), dev(dy=NY - 1)
    sent = []

    def copy(src, dst, sem, to):
        return pltpu.make_async_remote_copy(
            src_ref=src, dst_ref=dst, send_sem=ss.at[sem], recv_sem=rs.at[sem],
            device_id=to, device_id_type=MESH,
        )

    def send(src, dst, sem, to):
        cp = copy(src, dst, sem, to)
        cp.start()
        sent.append(cp)

    def arrive(dst, sem, frm):
        copy(dst, dst, sem, frm).wait_recv()

    def signal(sem, to):
        pl.semaphore_signal(sem, inc=1, device_id=to, device_id_type=MESH)

    barrier = pltpu.get_barrier_semaphore()
    greet = [sib, xp, xm, yp, ym] + [dev(dzl=k) for k in range(1, NZ)]
    for to in greet:
        signal(barrier, to)
    low, high = zl == 0, zl == NZ - 1
    below, above = dev(dzh=1, dzl=NZ - 1), dev(dzh=1, dzl=1)

    @pl.when(low)
    def _():
        signal(barrier, below)
        pl.semaphore_wait(barrier, len(greet) + 1)

    @pl.when(high)
    def _():
        signal(barrier, above)
        pl.semaphore_wait(barrier, len(greet) + 1)

    @pl.when(jnp.logical_and(zl > 0, zl < NZ - 1))
    def _():
        pl.semaphore_wait(barrier, len(greet))

    chunk_of = [zl, zl + 1 - 2 * (zl % 2), (zl + 2) % NZ, NZ - 1 - zl]

    def zdev(t):
        return (chunk_of[t] * NY + y, u)

    def pblock(t, dy):
        return ptb.at[c, chunk_of[t], up(dy)]

    for t in range(1, NZ):
        send(pt_ref, pblock(0, 0), PZ + t, zdev(t))
    send(pt_ref, pblock(0, 0), PYP, yp)
    send(pt_ref, pblock(0, 0), PYM, ym)

    def fcol(m, core):
        return pl.ds(pl.multiple_of((2 * m + core) * BLK, BLK), BLK)

    for m in range(8):
        send(f_ref.at[:, fcol(m, 1 - c)], fr.at[m], FS + m, sib)

    @pl.when(low)
    def _():
        signal(near, below)

    @pl.when(high)
    def _():
        signal(near, above)

    ptb[c, zl, y] = pt_ref[...]

    for z in range(NZ):
        row = jnp.broadcast_to(ve_ref[:, z * 256:(z + 1) * 256], (BLK, 256))
        vcol[z] = row.T
    vrow = ve_ref[:, pl.ds(pl.multiple_of((x * 2 + c) * BLK, BLK), BLK)]
    shift = occ_ref[zh] + pe_ref[0]

    def partner_z(t):
        b = pblock(t, 0)
        arrive(b, PZ + t, zdev(t))
        send(b, b, PYP + t, yp)
        send(b, b, PYM + t, ym)

    def half(b, n):
        return b.at[pl.ds(32 * n, 32)]

    def partner_side(t):
        b = pblock(t, NY - 1)
        arrive(b, PYP + t, ym)
        send(half(b, 0), half(b, 0), PFP + t, yp)
        b = pblock(t, 1)
        arrive(b, PYM + t, yp)
        send(half(b, 1), half(b, 1), PFM + t, ym)

    def partner_far(t):
        b = pblock(t, 2)
        arrive(half(b, 0), PFP + t, ym)
        arrive(half(b, 1), PFM + t, yp)
        row = chunk_of[t]
        send(ptb.at[c, row], ptb.at[c, row], PS + t, sib)

    def spot(h, dx):
        return h * NX + (x + dx) % NX

    def partial(t):
        row = chunk_of[t]
        arrive(ptb.at[1 - c, row], PS + t, sib)

        @pl.loop(0, 4)
        def _(pair):
            mine = ptb[c, row].reshape(256, 512)
            other = ptb[1 - c, row].reshape(256, 512)
            f_mine = jnp.concatenate(
                [f_ref[:, fcol(2 * pair, c)], f_ref[:, fcol(2 * pair + 1, c)]], axis=1
            )
            f_other = jnp.concatenate([fr[2 * pair], fr[2 * pair + 1]], axis=1)
            total = jnp.dot(mine, f_mine, preferred_element_type=jnp.float32)
            total += jnp.dot(other, f_other, preferred_element_type=jnp.float32)
            total = total.astype(jnp.bfloat16)
            part[t, 2 * pair] = total[:, :BLK]
            part[t, 2 * pair + 1] = total[:, BLK:]

        send(part.at[t, spot(0, 2)], rx1.at[t, 0], R1 + 2 * t, xp)
        send(part.at[t, spot(1, 2)], rx1.at[t, 1], R1 + 2 * t + 1, xm)
        send(part.at[t, spot(1, 1)], rx2.at[t, 1], R2 + 4 * t + 1, xp)
        send(part.at[t, spot(0, NX - 1)], rx2.at[t, 2], R2 + 4 * t + 2, xm)

    def combine(t):
        for h, dx, to, frm, slot in ((0, 1, xp, xm, 0), (1, NX - 1, xm, xp, 3)):
            arrive(rx1.at[t, h], R1 + 2 * t + h, frm)
            m = spot(h, dx)
            both = part[t, m].astype(jnp.float32) + rx1[t, h].astype(jnp.float32)
            part[t, m] = both.astype(jnp.bfloat16)
            send(part.at[t, m], rx2.at[t, slot], R2 + 4 * t + slot, to)

    def over_x(t):
        for slot in range(4):
            arrive(rx2.at[t, slot], R2 + 4 * t + slot, xm if slot < 2 else xp)

        def total(h):
            return (
                part[t, spot(h, 0)].astype(jnp.float32)
                + rx2[t, h].astype(jnp.float32)
                + rx2[t, 2 + h].astype(jnp.float32)
            )

        part[t, spot(1 - zh, 0)] = total(1 - zh).astype(jnp.bfloat16)
        send(part.at[t, spot(1 - zh, 0)], zr.at[t], RZ + t, zpart)
        keep[t] = total(zh)

    step = 1 - 2 * zh

    def ablock(h, dx, row):
        return at.at[c, spot(h, dx), row]

    def amplitude(t):
        row = chunk_of[t]
        arrive(zr.at[t], RZ + t, zpart)
        total = keep[t] + zr[t].astype(jnp.float32)
        divisor = vrow + vcol[row] - shift
        amp = (-total / divisor).astype(jnp.bfloat16)
        at[c, spot(zh, 0), row] = amp
        b = ablock(zh, 0, row)
        send(b, b, GX + 4 * t, xp)
        send(b, b, GX + 4 * t + 1, xm)
        send(b, b, GZ + t, zpart)

    def gather_z(t):
        b = ablock(1 - zh, 0, chunk_of[t])
        arrive(b, GZ + t, zpart)
        send(b, b, GX + 4 * t + 2, xp)
        send(b, b, GX + 4 * t + 3, xm)

    def gather_own(t):
        row = chunk_of[t]
        arrive(ablock(zh, NX - 1, row), GX + 4 * t, xm)
        arrive(ablock(zh, 1, row), GX + 4 * t + 1, xp)
        b = ablock(zh, NX - step, row)
        send(b, b, GF + 2 * t, dev(dx=NX + step))

    def gather_other(t):
        row = chunk_of[t]
        arrive(ablock(1 - zh, NX - 1, row), GX + 4 * t + 2, xm)
        arrive(ablock(1 - zh, 1, row), GX + 4 * t + 3, xp)
        b = ablock(1 - zh, NX + step, row)
        send(b, b, GF + 2 * t + 1, dev(dx=NX - step))

    def gather_end(t):
        row = chunk_of[t]
        arrive(ablock(zh, 2, row), GF + 2 * t, dev(dx=NX - step))
        arrive(ablock(1 - zh, 2, row), GF + 2 * t + 1, dev(dx=NX + step))
        send(at.at[c, :, row], at.at[c, :, row], GS + t, sib)

    partner_side(0)
    partner_z(1)
    partner_far(0)
    partner_z(2)
    partner_side(1)
    for m in range(8):
        arrive(fr.at[m], FS + m, sib)
    partial(0)
    partner_z(3)
    partner_far(1)
    partner_side(2)
    partial(1)
    combine(0)
    partner_far(2)
    partner_side(3)
    partial(2)
    combine(1)

    @pl.when(low)
    def _():
        pl.semaphore_wait(near, 1)
        signal(near, dev(dzl=1))
        signal(near, dev(dzl=2))

    @pl.when(zl > 0)
    def _():
        pl.semaphore_wait(near, 1)

    over_x(0)
    partner_far(3)
    partial(3)
    combine(2)
    over_x(1)
    combine(3)

    for z in range(NZ):
        ptrue[:, z * 256:(z + 1) * 256] = ptb[c, z].reshape(256, 512).T

    amplitude(0)
    over_x(2)
    amplitude(1)
    gather_own(0)
    over_x(3)
    gather_z(0)
    gather_own(1)
    amplitude(2)
    gather_other(0)
    gather_z(1)
    gather_own(2)
    amplitude(3)
    gather_end(0)
    gather_other(1)
    gather_z(2)
    gather_own(3)
    gather_end(1)
    gather_other(2)
    gather_z(3)
    for z in range(NZ):
        amp_ref[:, z * 256:(z + 1) * 256] = at[c, spot(zh, 0), z].T
    gather_end(2)
    gather_other(3)
    gather_end(3)
    for t in range(4):
        row = chunk_of[t]
        arrive(at.at[1 - c, :, row], GS + t, sib)

    @pl.loop(0, 2)
    def _(i):
        for z in range(NX):
            wide = jnp.concatenate(
                [at[0, i * NX + z].reshape(1024, BLK), at[1, i * NX + z].reshape(1024, BLK)], axis=1
            )
            direct = jnp.dot(ptrue[...], wide, preferred_element_type=jnp.float32)
            tall = jnp.concatenate(
                [at[j % 2, i * NX + j // 2, z] for j in range(2 * NX)], axis=1
            )
            swapped = lax.dot_general(
                ptrue[...], tall, (((1,), (1,)), ((), ())), preferred_element_type=jnp.float32
            )
            den_ref[i, :, z * 256:(z + 1) * 256] = (2.0 * direct - swapped).astype(jnp.bfloat16)

    for cp in sent:
        cp.wait_send()


def shards(factors, partner, occupied_energy, partner_energy, virtual_energy):
    bf = jnp.bfloat16
    vmem = pl.BlockSpec(memory_space=pltpu.VMEM)
    smem = pl.BlockSpec(memory_space=pltpu.SMEM)
    amp, den = pl.pallas_call(
        kernel,
        out_shape=(jax.ShapeDtypeStruct((BLK, 1024), bf), jax.ShapeDtypeStruct((2, 512, 1024), bf)),
        in_specs=[vmem, vmem, smem, smem, vmem],
        out_specs=(vmem, vmem),
        scratch_shapes=[
            pltpu.VMEM((2, NZ, NY, 64, 512), bf),
            pltpu.VMEM((8, 512, BLK), bf),
            pltpu.VMEM((4, 8, 256, BLK), bf),
            pltpu.VMEM((4, 2, 256, BLK), bf),
            pltpu.VMEM((4, 4, 256, BLK), bf),
            pltpu.VMEM((4, 256, BLK), jnp.float32),
            pltpu.VMEM((4, 256, BLK), bf),
            pltpu.VMEM((2, 8, NZ, 256, BLK), bf),
            pltpu.VMEM((4, 256, BLK), jnp.float32),
            pltpu.VMEM((512, 1024), bf),
            pltpu.SemaphoreType.DMA((NSEM,)),
            pltpu.SemaphoreType.DMA((NSEM,)),
            pltpu.SemaphoreType.REGULAR,
        ],
        compiler_params=pltpu.CompilerParams(
            collective_id=0, has_side_effects=True, vmem_limit_bytes=48 << 20
        ),
    )(factors.reshape(512, 2048), partner.T, occupied_energy, partner_energy, virtual_energy.reshape(1, 1024))
    return amp, den.transpose(1, 0, 2)


def solution(mesh):
    return jax.shard_map(
        shards,
        mesh=mesh,
        in_specs=(P("aux", "occ", None), P("aux", "occ"), P("occ"), P(), P()),
        out_specs=(P(("occ", "aux"), None), P("aux", "occ", None)),
        check_vma=False,
    )
```

```python
import jax
import jax.numpy as jnp
from jax import lax
from jax.experimental import pallas as pl
from jax.experimental.pallas import tpu as pltpu
from jax.sharding import PartitionSpec as P

MESH = pl.DeviceIdType.MESH
GRID = 2
NX, NY, NZ = 4, 4, 4
BLK = 128

PZ = 0
PYP = 4
PYM = 8
PFP = 12
PFM = 16
PS = 20
FS = 24
R1 = 32
R2 = 40
RZ = 56
GX = 64
GF = 80
GS = 88
GL = 92
NSEM = 100


def kernel(
    f_ref, pt_ref, occ_ref, pe_ref, ve_ref,
    amp_ref, at, ptrue,
    ptb, fr, part, rx1, rx2, zs, zr, vcol, ss, rs, near,
):
    o, u = lax.axis_index("occ"), lax.axis_index("aux")
    zl, y = o // NY, o % NY
    zh, x, c = u // (2 * NX), (u // 2) % NX, u % 2

    def up(k):
        return (y + k) % NY

    def dev(dzh=0, dzl=0, dy=0, dx=0, dc=0):
        return (
            ((zl + dzl) % NZ) * NY + (y + dy) % NY,
            (((zh + dzh) % 2) * NX + (x + dx) % NX) * 2 + (c + dc) % 2,
        )

    sib, zpart = dev(dc=1), dev(dzh=1)
    xp, xm = dev(dx=1), dev(dx=NX - 1)
    yp, ym = dev(dy=1), dev(dy=NY - 1)
    sent = []

    def copy(src, dst, sem, to):
        return pltpu.make_async_remote_copy(
            src_ref=src, dst_ref=dst, send_sem=ss.at[sem], recv_sem=rs.at[sem],
            device_id=to, device_id_type=MESH,
        )

    def send(src, dst, sem, to):
        cp = copy(src, dst, sem, to)
        cp.start()
        sent.append(cp)

    def arrive(dst, sem, frm):
        copy(dst, dst, sem, frm).wait_recv()

    def signal(sem, to):
        pl.semaphore_signal(sem, inc=1, device_id=to, device_id_type=MESH)

    barrier = pltpu.get_barrier_semaphore()
    greet = [sib, xp, xm, yp, ym] + [dev(dzl=k) for k in range(1, NZ)]
    for to in greet:
        signal(barrier, to)
    low, high = zl == 0, zl == NZ - 1
    below, above = dev(dzh=1, dzl=NZ - 1), dev(dzh=1, dzl=1)

    @pl.when(low)
    def _():
        signal(barrier, below)
        pl.semaphore_wait(barrier, len(greet) + 1)

    @pl.when(high)
    def _():
        signal(barrier, above)
        pl.semaphore_wait(barrier, len(greet) + 1)

    @pl.when(jnp.logical_and(zl > 0, zl < NZ - 1))
    def _():
        pl.semaphore_wait(barrier, len(greet))

    chunk_of = [zl, zl + 1 - 2 * (zl % 2), (zl + 2) % NZ, NZ - 1 - zl]

    def zdev(t):
        return (chunk_of[t] * NY + y, u)

    def pblock(t, dy):
        return ptb.at[c, chunk_of[t], up(dy)]

    for t in range(1, NZ):
        send(pt_ref, pblock(0, 0), PZ + t, zdev(t))
    send(pt_ref, pblock(0, 0), PYP, yp)
    send(pt_ref, pblock(0, 0), PYM, ym)

    def fcol(m, core):
        return pl.ds(pl.multiple_of((2 * m + core) * BLK, BLK), BLK)

    for m in range(8):
        send(f_ref.at[:, fcol(m, 1 - c)], fr.at[m], FS + m, sib)

    @pl.when(low)
    def _():
        signal(near, below)

    @pl.when(high)
    def _():
        signal(near, above)

    ptb[c, zl, y] = pt_ref[...]

    vrow = ve_ref[:, pl.ds(pl.multiple_of((x * 2 + c) * BLK, BLK), BLK)]

    def partner_z(t):
        b = pblock(t, 0)
        arrive(b, PZ + t, zdev(t))
        send(b, b, PYP + t, yp)
        send(b, b, PYM + t, ym)

    def half(b, n):
        return b.at[pl.ds(32 * n, 32)]

    def partner_side(t):
        b = pblock(t, NY - 1)
        arrive(b, PYP + t, ym)
        send(half(b, 0), half(b, 0), PFP + t, yp)
        b = pblock(t, 1)
        arrive(b, PYM + t, yp)
        send(half(b, 1), half(b, 1), PFM + t, ym)

    def partner_far(t):
        b = pblock(t, 2)
        arrive(half(b, 0), PFP + t, ym)
        arrive(half(b, 1), PFM + t, yp)
        row = chunk_of[t]
        send(ptb.at[c, row], ptb.at[c, row], PS + t, sib)

    def spot(h, dx):
        return h * NX + (x + dx) % NX

    def partial(t):
        row = chunk_of[t]
        arrive(ptb.at[1 - c, row], PS + t, sib)

        @pl.loop(0, 4)
        def _(pair):
            mine = ptb[c, row].reshape(256, 512)
            other = ptb[1 - c, row].reshape(256, 512)
            f_mine = jnp.concatenate(
                [f_ref[:, fcol(2 * pair, c)], f_ref[:, fcol(2 * pair + 1, c)]], axis=1
            )
            f_other = jnp.concatenate([fr[2 * pair], fr[2 * pair + 1]], axis=1)
            total = jnp.dot(mine, f_mine, preferred_element_type=jnp.float32)
            total += jnp.dot(other, f_other, preferred_element_type=jnp.float32)
            total = total.astype(jnp.bfloat16)
            part[t, 2 * pair] = total[:, :BLK]
            part[t, 2 * pair + 1] = total[:, BLK:]

        send(part.at[t, spot(0, 2)], rx1.at[t, 0], R1 + 2 * t, xp)
        send(part.at[t, spot(1, 2)], rx1.at[t, 1], R1 + 2 * t + 1, xm)
        send(part.at[t, spot(1, 1)], rx2.at[t, 1], R2 + 4 * t + 1, xp)
        send(part.at[t, spot(0, NX - 1)], rx2.at[t, 2], R2 + 4 * t + 2, xm)

    def combine(t):
        for h, dx, to, frm, slot in ((0, 1, xp, xm, 0), (1, NX - 1, xm, xp, 3)):
            arrive(rx1.at[t, h], R1 + 2 * t + h, frm)
            m = spot(h, dx)
            both = part[t, m].astype(jnp.float32) + rx1[t, h].astype(jnp.float32)
            part[t, m] = both.astype(jnp.bfloat16)
            send(part.at[t, m], rx2.at[t, slot], R2 + 4 * t + slot, to)

    def over_x(t):
        for slot in range(4):
            arrive(rx2.at[t, slot], R2 + 4 * t + slot, xm if slot < 2 else xp)

        for h in range(2):
            total = (
                part[t, spot(h, 0)].astype(jnp.float32)
                + rx2[t, h].astype(jnp.float32)
                + rx2[t, 2 + h].astype(jnp.float32)
            )
            zs[t, h] = total.astype(jnp.bfloat16)
        send(zs.at[t], zr.at[t], RZ + t, zpart)

    def ablock(h, dx, row):
        return at.at[c, spot(h, dx), row]

    def amplitude(t):
        row = chunk_of[t]
        arrive(zr.at[t], RZ + t, zpart)
        for h in range(2):
            total = zs[t, h].astype(jnp.float32) + zr[t, h].astype(jnp.float32)
            divisor = vrow + vcol[row] - (occ_ref[h] + pe_ref[0])
            at[c, spot(h, 0), row] = (-total / divisor).astype(jnp.bfloat16)
        for h, to, n in ((0, xp, 0), (1, xm, 1), (1, xp, 2), (0, xm, 3)):
            send(ablock(h, 0, row), ablock(h, 0, row), GX + 4 * t + n, to)
        hand_over(t, ((0, 0), (1, 0)))

    def hand_over(t, blocks):
        if t == 3:
            for h, dx in blocks:
                b = ablock(h, dx, chunk_of[t])
                send(b, b, GL + h * NX + dx, sib)

    def forward(t):
        row = chunk_of[t]
        arrive(ablock(0, NX - 1, row), GX + 4 * t, xm)
        send(ablock(0, NX - 1, row), ablock(0, NX - 1, row), GF + 2 * t, xp)
        arrive(ablock(1, 1, row), GX + 4 * t + 1, xp)
        send(ablock(1, 1, row), ablock(1, 1, row), GF + 2 * t + 1, xm)
        hand_over(t, ((0, NX - 1), (1, 1)))

    def gather_end(t):
        row = chunk_of[t]
        arrive(ablock(1, NX - 1, row), GX + 4 * t + 2, xm)
        arrive(ablock(0, 1, row), GX + 4 * t + 3, xp)
        hand_over(t, ((1, NX - 1), (0, 1)))
        arrive(ablock(0, 2, row), GF + 2 * t, xm)
        arrive(ablock(1, 2, row), GF + 2 * t + 1, xp)
        hand_over(t, ((0, 2), (1, 2)))
        if t < 3:
            send(at.at[c, :, row], at.at[c, :, row], GS + t, sib)

    def from_sibling(t):
        row = chunk_of[t]
        if t < 3:
            arrive(at.at[1 - c, :, row], GS + t, sib)
            return
        for h in range(2):
            for dx in range(NX):
                arrive(at.at[1 - c, spot(h, dx), row], GL + h * NX + dx, sib)

    def columns_of_energy():
        for z in range(NZ):
            row = jnp.broadcast_to(ve_ref[:, z * 256:(z + 1) * 256], (BLK, 256))
            vcol[z] = row.T

    def turned_partner():
        for z in range(NZ):
            ptrue[:, z * 256:(z + 1) * 256] = ptb[c, z].reshape(256, 512).T

    def own_amplitudes():
        for z in range(NZ):
            amp_ref[:, z * 256:(z + 1) * 256] = at[c, spot(zh, 0), z].T

    def far_run():
        @pl.when(low)
        def _():
            pl.semaphore_wait(near, 1)
            signal(near, dev(dzl=1))
            signal(near, dev(dzl=2))

        @pl.when(zl > 0)
        def _():
            pl.semaphore_wait(near, 1)

    partner_side(0)
    partner_z(1)
    partner_far(0)
    partner_z(2)
    for m in range(8):
        arrive(fr.at[m], FS + m, sib)
    partial(0)
    partner_side(1)
    partner_z(3)
    far_run()
    partner_far(1)
    partner_side(2)
    combine(0)
    partial(1)
    over_x(0)
    partner_side(3)
    partner_far(2)
    combine(1)
    partial(2)
    partner_far(3)
    over_x(1)
    partial(3)
    combine(2)
    columns_of_energy()
    over_x(2)
    combine(3)
    amplitude(0)
    over_x(3)
    turned_partner()
    forward(0)
    amplitude(1)
    gather_end(0)
    forward(1)
    amplitude(2)
    gather_end(1)
    forward(2)
    amplitude(3)
    gather_end(2)
    forward(3)
    own_amplitudes()
    gather_end(3)
    for t in range(4):
        from_sibling(t)

    for cp in sent:
        cp.wait_send()


def density(amp_in, at, ptrue, amp_ref, den_ref):
    g, lines = pl.program_id(0), den_ref.shape[0]
    amp_rows = amp_ref.shape[0]
    amp_ref[...] = amp_in[pl.ds(pl.multiple_of(g * amp_rows, amp_rows), amp_rows)]
    mine = ptrue[pl.ds(pl.multiple_of(g * lines, lines), lines)]
    for z in range(NX):
        for i in range(2):
            wide = jnp.concatenate(
                [at[k, i * NX + z].reshape(1024, BLK) for k in range(2)], axis=1
            )
            direct = jnp.dot(mine, wide, preferred_element_type=jnp.float32)
            tall = jnp.concatenate(
                [at[j % 2, i * NX + j // 2, z] for j in range(2 * NX)], axis=1
            )
            swapped = lax.dot_general(
                mine, tall, (((1,), (1,)), ((), ())), preferred_element_type=jnp.float32
            )
            den_ref[:, i, z * 256:(z + 1) * 256] = (2.0 * direct - swapped).astype(jnp.bfloat16)


def shards(factors, partner, occupied_energy, partner_energy, virtual_energy):
    bf = jnp.bfloat16
    vmem = pl.BlockSpec(memory_space=pltpu.VMEM)
    smem = pl.BlockSpec(memory_space=pltpu.SMEM)
    amp, at, ptrue = pl.pallas_call(
        kernel,
        out_shape=(
            jax.ShapeDtypeStruct((BLK, 1024), bf),
            jax.ShapeDtypeStruct((2, 8, NZ, 256, BLK), bf),
            jax.ShapeDtypeStruct((512, 1024), bf),
        ),
        in_specs=[vmem, vmem, smem, smem, vmem],
        out_specs=(vmem, vmem, vmem),
        scratch_shapes=[
            pltpu.VMEM((2, NZ, NY, 64, 512), bf),
            pltpu.VMEM((8, 512, BLK), bf),
            pltpu.VMEM((4, 8, 256, BLK), bf),
            pltpu.VMEM((4, 2, 256, BLK), bf),
            pltpu.VMEM((4, 4, 256, BLK), bf),
            pltpu.VMEM((4, 2, 256, BLK), bf),
            pltpu.VMEM((4, 2, 256, BLK), bf),
            pltpu.VMEM((4, 256, BLK), jnp.float32),
            pltpu.SemaphoreType.DMA((NSEM,)),
            pltpu.SemaphoreType.DMA((NSEM,)),
            pltpu.SemaphoreType.REGULAR,
        ],
        compiler_params=pltpu.CompilerParams(
            collective_id=0, has_side_effects=True, vmem_limit_bytes=24 << 20
        ),
    )(factors.reshape(512, 2048), partner.T, occupied_energy, partner_energy, virtual_energy.reshape(1, 1024))
    steps = GRID
    return pl.pallas_call(
        density,
        grid=(steps,),
        out_shape=(
            jax.ShapeDtypeStruct((BLK, 1024), bf),
            jax.ShapeDtypeStruct((512, 2, 1024), bf),
        ),
        in_specs=[vmem, vmem, vmem],
        out_specs=(
            pl.BlockSpec((BLK // steps, 1024), lambda g: (g, 0)),
            pl.BlockSpec((512 // steps, 2, 1024), lambda g: (g, 0, 0)),
        ),
        compiler_params=pltpu.CompilerParams(vmem_limit_bytes=20 << 20),
    )(amp, at, ptrue)


def solution(mesh):
    return jax.shard_map(
        shards,
        mesh=mesh,
        in_specs=(P("aux", "occ", None), P("aux", "occ"), P("occ"), P(), P()),
        out_specs=(P(("occ", "aux"), None), P("aux", "occ", None)),
        check_vma=False,
    )
```

```python
import jax
import jax.numpy as jnp
from jax import lax
from jax.experimental import pallas as pl
from jax.experimental.pallas import tpu as pltpu
from jax.sharding import PartitionSpec as P

MESH = pl.DeviceIdType.MESH
GRID = 2
NX, NY, NZ = 4, 4, 4
BLK = 128

PZ = 0
PYP = 4
PYM = 8
PFP = 12
PFM = 16
PS = 20
FS = 24
R1 = 32
R2 = 40
RZ = 56
GX = 64
GF = 80
GS = 88
GL = 92
NSEM = 100


def kernel(
    f_ref, pt_ref, occ_ref, pe_ref, ve_ref,
    amp_ref, at, ptrue,
    ptb, fr, part, rx1, rx2, zs, zr, vcol, ss, rs, near,
):
    o, u = lax.axis_index("occ"), lax.axis_index("aux")
    zl, y = o // NY, o % NY
    zh, x, c = u // (2 * NX), (u // 2) % NX, u % 2

    def up(k):
        return (y + k) % NY

    def dev(dzh=0, dzl=0, dy=0, dx=0, dc=0):
        return (
            ((zl + dzl) % NZ) * NY + (y + dy) % NY,
            (((zh + dzh) % 2) * NX + (x + dx) % NX) * 2 + (c + dc) % 2,
        )

    sib, zpart = dev(dc=1), dev(dzh=1)
    xp, xm = dev(dx=1), dev(dx=NX - 1)
    yp, ym = dev(dy=1), dev(dy=NY - 1)
    sent = []

    def copy(src, dst, sem, to):
        return pltpu.make_async_remote_copy(
            src_ref=src, dst_ref=dst, send_sem=ss.at[sem], recv_sem=rs.at[sem],
            device_id=to, device_id_type=MESH,
        )

    def send(src, dst, sem, to):
        cp = copy(src, dst, sem, to)
        cp.start()
        sent.append(cp)

    def arrive(dst, sem, frm):
        copy(dst, dst, sem, frm).wait_recv()

    def signal(sem, to):
        pl.semaphore_signal(sem, inc=1, device_id=to, device_id_type=MESH)

    barrier = pltpu.get_barrier_semaphore()
    greet = [sib, xp, xm, yp, ym] + [dev(dzl=k) for k in range(1, NZ)]
    for to in greet:
        signal(barrier, to)
    low, high = zl == 0, zl == NZ - 1
    below, above = dev(dzh=1, dzl=NZ - 1), dev(dzh=1, dzl=1)

    @pl.when(low)
    def _():
        signal(barrier, below)
        pl.semaphore_wait(barrier, len(greet) + 1)

    @pl.when(high)
    def _():
        signal(barrier, above)
        pl.semaphore_wait(barrier, len(greet) + 1)

    @pl.when(jnp.logical_and(zl > 0, zl < NZ - 1))
    def _():
        pl.semaphore_wait(barrier, len(greet))

    chunk_of = [zl, zl + 1 - 2 * (zl % 2), (zl + 2) % NZ, NZ - 1 - zl]

    def zdev(t):
        return (chunk_of[t] * NY + y, u)

    def pblock(t, dy):
        return ptb.at[c, chunk_of[t], up(dy)]

    for t in range(1, NZ):
        send(pt_ref, pblock(0, 0), PZ + t, zdev(t))
    send(pt_ref, pblock(0, 0), PYP, yp)
    send(pt_ref, pblock(0, 0), PYM, ym)

    def fcol(m, core):
        return pl.ds(pl.multiple_of((2 * m + core) * BLK, BLK), BLK)

    for m in range(8):
        send(f_ref.at[:, fcol(m, 1 - c)], fr.at[m], FS + m, sib)

    @pl.when(low)
    def _():
        signal(near, below)

    @pl.when(high)
    def _():
        signal(near, above)

    ptb[c, zl, y] = pt_ref[...]

    vrow = ve_ref[:, pl.ds(pl.multiple_of((x * 2 + c) * BLK, BLK), BLK)]

    def partner_z(t):
        b = pblock(t, 0)
        arrive(b, PZ + t, zdev(t))
        send(b, b, PYP + t, yp)
        send(b, b, PYM + t, ym)

    def half(b, n):
        return b.at[pl.ds(32 * n, 32)]

    def partner_side(t):
        b = pblock(t, NY - 1)
        arrive(b, PYP + t, ym)
        send(half(b, 0), half(b, 0), PFP + t, yp)
        b = pblock(t, 1)
        arrive(b, PYM + t, yp)
        send(half(b, 1), half(b, 1), PFM + t, ym)

    def partner_far(t):
        b = pblock(t, 2)
        arrive(half(b, 0), PFP + t, ym)
        arrive(half(b, 1), PFM + t, yp)
        row = chunk_of[t]
        send(ptb.at[c, row], ptb.at[c, row], PS + t, sib)

    def spot(h, dx):
        return h * NX + (x + dx) % NX

    def partial(t):
        row = chunk_of[t]
        arrive(ptb.at[1 - c, row], PS + t, sib)

        @pl.loop(0, 4)
        def _(pair):
            mine = ptb[c, row].reshape(256, 512)
            other = ptb[1 - c, row].reshape(256, 512)
            f_mine = jnp.concatenate(
                [f_ref[:, fcol(2 * pair, c)], f_ref[:, fcol(2 * pair + 1, c)]], axis=1
            )
            f_other = jnp.concatenate([fr[2 * pair], fr[2 * pair + 1]], axis=1)
            total = jnp.dot(mine, f_mine, preferred_element_type=jnp.float32)
            total += jnp.dot(other, f_other, preferred_element_type=jnp.float32)
            total = total.astype(jnp.bfloat16)
            part[t, 2 * pair] = total[:, :BLK]
            part[t, 2 * pair + 1] = total[:, BLK:]

        send(part.at[t, spot(0, 2)], rx1.at[t, 0], R1 + 2 * t, xp)
        send(part.at[t, spot(1, 2)], rx1.at[t, 1], R1 + 2 * t + 1, xm)
        send(part.at[t, spot(1, 1)], rx2.at[t, 1], R2 + 4 * t + 1, xp)
        send(part.at[t, spot(0, NX - 1)], rx2.at[t, 2], R2 + 4 * t + 2, xm)

    def combine(t):
        for h, dx, to, frm, slot in ((0, 1, xp, xm, 0), (1, NX - 1, xm, xp, 3)):
            arrive(rx1.at[t, h], R1 + 2 * t + h, frm)
            m = spot(h, dx)
            both = part[t, m].astype(jnp.float32) + rx1[t, h].astype(jnp.float32)
            part[t, m] = both.astype(jnp.bfloat16)
            send(part.at[t, m], rx2.at[t, slot], R2 + 4 * t + slot, to)

    def over_x(t):
        for slot in range(4):
            arrive(rx2.at[t, slot], R2 + 4 * t + slot, xm if slot < 2 else xp)

        for h in range(2):
            total = (
                part[t, spot(h, 0)].astype(jnp.float32)
                + rx2[t, h].astype(jnp.float32)
                + rx2[t, 2 + h].astype(jnp.float32)
            )
            zs[t, h] = total.astype(jnp.bfloat16)
        send(zs.at[t], zr.at[t], RZ + t, zpart)

    def ablock(h, dx, row):
        return at.at[c, spot(h, dx), row]

    def amplitude(t):
        row = chunk_of[t]
        arrive(zr.at[t], RZ + t, zpart)
        for h in range(2):
            total = zs[t, h].astype(jnp.float32) + zr[t, h].astype(jnp.float32)
            divisor = vrow + vcol[row] - (occ_ref[h] + pe_ref[0])
            at[c, spot(h, 0), row] = (-total / divisor).astype(jnp.bfloat16)
        for h, to, n in ((0, xp, 0), (1, xm, 1), (1, xp, 2), (0, xm, 3)):
            send(ablock(h, 0, row), ablock(h, 0, row), GX + 4 * t + n, to)
        hand_over(t, ((0, 0), (1, 0)))

    def hand_over(t, blocks):
        if t == 3:
            for h, dx in blocks:
                b = ablock(h, dx, chunk_of[t])
                send(b, b, GL + h * NX + dx, sib)

    def forward(t):
        row = chunk_of[t]
        arrive(ablock(0, NX - 1, row), GX + 4 * t, xm)
        send(ablock(0, NX - 1, row), ablock(0, NX - 1, row), GF + 2 * t, xp)
        arrive(ablock(1, 1, row), GX + 4 * t + 1, xp)
        send(ablock(1, 1, row), ablock(1, 1, row), GF + 2 * t + 1, xm)
        hand_over(t, ((0, NX - 1), (1, 1)))

    def gather_end(t):
        row = chunk_of[t]
        arrive(ablock(1, NX - 1, row), GX + 4 * t + 2, xm)
        arrive(ablock(0, 1, row), GX + 4 * t + 3, xp)
        hand_over(t, ((1, NX - 1), (0, 1)))
        arrive(ablock(0, 2, row), GF + 2 * t, xm)
        arrive(ablock(1, 2, row), GF + 2 * t + 1, xp)
        hand_over(t, ((0, 2), (1, 2)))
        if t < 3:
            send(at.at[c, :, row], at.at[c, :, row], GS + t, sib)

    def from_sibling(t):
        row = chunk_of[t]
        if t < 3:
            arrive(at.at[1 - c, :, row], GS + t, sib)
            return
        for h in range(2):
            for dx in range(NX):
                arrive(at.at[1 - c, spot(h, dx), row], GL + h * NX + dx, sib)

    def columns_of_energy():
        for z in range(NZ):
            row = jnp.broadcast_to(ve_ref[:, z * 256:(z + 1) * 256], (BLK, 256))
            vcol[z] = row.T

    def turned_partner():
        for z in range(NZ):
            ptrue[:, z * 256:(z + 1) * 256] = ptb[c, z].reshape(256, 512).T

    def own_amplitudes():
        for z in range(NZ):
            amp_ref[:, z * 256:(z + 1) * 256] = at[c, spot(zh, 0), z].T

    def far_run():
        @pl.when(low)
        def _():
            pl.semaphore_wait(near, 1)
            signal(near, dev(dzl=1))
            signal(near, dev(dzl=2))

        @pl.when(zl > 0)
        def _():
            pl.semaphore_wait(near, 1)

    partner_z(1)
    partner_side(0)
    partner_z(2)
    partner_far(0)
    for m in range(8):
        arrive(fr.at[m], FS + m, sib)
    partial(0)
    partner_z(3)
    partner_side(1)
    far_run()
    partner_far(1)
    partner_side(2)
    combine(0)
    partial(1)
    over_x(0)
    partner_side(3)
    partner_far(2)
    combine(1)
    partial(2)
    partner_far(3)
    over_x(1)
    partial(3)
    combine(2)
    columns_of_energy()
    over_x(2)
    combine(3)
    amplitude(0)
    over_x(3)
    amplitude(1)
    forward(0)
    forward(1)
    amplitude(2)
    gather_end(0)
    forward(2)
    gather_end(1)
    amplitude(3)
    turned_partner()
    gather_end(2)
    forward(3)
    own_amplitudes()
    gather_end(3)

    for t in range(4):
        from_sibling(t)

    for cp in sent:
        cp.wait_send()


def density(amp_in, at, ptrue, amp_ref, den_ref):
    g, lines = pl.program_id(0), den_ref.shape[0]
    amp_rows = amp_ref.shape[0]
    amp_ref[...] = amp_in[pl.ds(pl.multiple_of(g * amp_rows, amp_rows), amp_rows)]
    mine = ptrue[pl.ds(pl.multiple_of(g * lines, lines), lines)]
    for z in range(NX):
        for i in range(2):
            wide = jnp.concatenate(
                [at[k, i * NX + z].reshape(1024, BLK) for k in range(2)], axis=1
            )
            direct = jnp.dot(mine, wide, preferred_element_type=jnp.float32)
            tall = jnp.concatenate(
                [at[j % 2, i * NX + j // 2, z] for j in range(2 * NX)], axis=1
            )
            swapped = lax.dot_general(
                mine, tall, (((1,), (1,)), ((), ())), preferred_element_type=jnp.float32
            )
            den_ref[:, i, z * 256:(z + 1) * 256] = (2.0 * direct - swapped).astype(jnp.bfloat16)


def shards(factors, partner, occupied_energy, partner_energy, virtual_energy):
    bf = jnp.bfloat16
    vmem = pl.BlockSpec(memory_space=pltpu.VMEM)
    smem = pl.BlockSpec(memory_space=pltpu.SMEM)
    amp, at, ptrue = pl.pallas_call(
        kernel,
        out_shape=(
            jax.ShapeDtypeStruct((BLK, 1024), bf),
            jax.ShapeDtypeStruct((2, 8, NZ, 256, BLK), bf),
            jax.ShapeDtypeStruct((512, 1024), bf),
        ),
        in_specs=[vmem, vmem, smem, smem, vmem],
        out_specs=(vmem, vmem, vmem),
        scratch_shapes=[
            pltpu.VMEM((2, NZ, NY, 64, 512), bf),
            pltpu.VMEM((8, 512, BLK), bf),
            pltpu.VMEM((4, 8, 256, BLK), bf),
            pltpu.VMEM((4, 2, 256, BLK), bf),
            pltpu.VMEM((4, 4, 256, BLK), bf),
            pltpu.VMEM((4, 2, 256, BLK), bf),
            pltpu.VMEM((4, 2, 256, BLK), bf),
            pltpu.VMEM((4, 256, BLK), jnp.float32),
            pltpu.SemaphoreType.DMA((NSEM,)),
            pltpu.SemaphoreType.DMA((NSEM,)),
            pltpu.SemaphoreType.REGULAR,
        ],
        compiler_params=pltpu.CompilerParams(
            collective_id=0, has_side_effects=True, vmem_limit_bytes=24 << 20
        ),
    )(factors.reshape(512, 2048), partner.T, occupied_energy, partner_energy, virtual_energy.reshape(1, 1024))
    steps = GRID
    return pl.pallas_call(
        density,
        grid=(steps,),
        out_shape=(
            jax.ShapeDtypeStruct((BLK, 1024), bf),
            jax.ShapeDtypeStruct((512, 2, 1024), bf),
        ),
        in_specs=[vmem, vmem, vmem],
        out_specs=(
            pl.BlockSpec((BLK // steps, 1024), lambda g: (g, 0)),
            pl.BlockSpec((512 // steps, 2, 1024), lambda g: (g, 0, 0)),
        ),
        compiler_params=pltpu.CompilerParams(vmem_limit_bytes=20 << 20),
    )(amp, at, ptrue)


def solution(mesh):
    return jax.shard_map(
        shards,
        mesh=mesh,
        in_specs=(P("aux", "occ", None), P("aux", "occ"), P("occ"), P(), P()),
        out_specs=(P(("occ", "aux"), None), P("aux", "occ", None)),
        check_vma=False,
    )
```
